32 devices in a mesh: fsdp: 2 (over core), expert: 16 (over z, y, x).
Axes of the slice: x: 2, y: 2, z: 4, core: 2. Of those that a mesh axis runs over, the one named last changes fastest.
Arguments:
- tokens: bfloat16 [16384, 1536], P(('fsdp', 'expert')), may hold values from -6 to 6
- norm_attn: bfloat16 [1536], P('fsdp'), may hold values from 0.5 to 1.5
- w_qkv: bfloat16 [1536, 2560], P('fsdp'), may hold values from -0.15625 to 0.15625
- w_out: bfloat16 [1536, 1536], P('fsdp'), may hold values from -6 to 6
- norm_moe: bfloat16 [1536], P('fsdp'), may hold values from 0.5 to 1.5
- w_router: bfloat16 [1536, 16], P('fsdp'), may hold values from -0.15625 to 0.15625
- expert_in: bfloat16 [16, 1536, 1024], P('expert'), may hold values from -0.15625 to 0.15625
- expert_out: bfloat16 [16, 512, 1536], P('expert'), may hold values from -3 to 3
- routes: int32 [16384, 8], P(('fsdp', 'expert')), may hold values from 0 to 15, all different within a row; in each aligned block of 512 rows (0 to 511, 512 to 1023, ...) at most 288 rows name the same one
- segments: int32 [16384], P(('fsdp', 'expert')), may hold values from 0 to 3, as said below
- positions: int32 [16384], P(('fsdp', 'expert')), may hold values from 0 to 1999, as said below
- cotangent: bfloat16 [16384, 1536], P(('fsdp', 'expert')), may hold values from -6 to 6
Outputs:
- block_out: bfloat16 [16384, 1536], P(('fsdp', 'expert'))
- grad_tokens: float32 [16384, 1536], P(('fsdp', 'expert'))
- grad_norm_attn: float32 [1536], P('fsdp')
- grad_qkv: float32 [1536, 2560], P('fsdp')
- grad_out_proj: float32 [1536, 1536], P('fsdp')
- grad_norm_moe: float32 [1536], P('fsdp')
- grad_router: float32 [1536, 16], P('fsdp')
- grad_expert_in: float32 [16, 1536, 1024], P('expert', 'fsdp')
- grad_expert_out: float32 [16, 512, 1536], P('expert', None, 'fsdp')
The draws below stay inside these ranges and needn't reach their ends.
Inputs may be any that keep to these rules, and one draw needn't show every extreme that they name: `routes`: in each aligned block of 512 rows (the rows of one device) no expert is named more than 288 times; the 8 experts of a row differ. `segments`: within each sequence of 512 tokens the numbers start at 0 and rise by one where a document begins; documents after a sequence's first hold 200 or more tokens. `positions`: A token's place in its document: it rises by one from token to token within a document and is 0 at each document's first token; a sequence's first document may have begun before the sequence; a document holds at most 2000 tokens.
All inputs are finite; a program needn't handle non-finite values.
Results may differ from the reference program's by a relative error of at most 0.02.
Values may be sent and summed in bfloat16 or wider, within the bound.
No kernel may reach another device: no remote copies, remote signals or barrier semaphores. Data moves between devices by JAX's collectives and lax.ppermute only.
A program may use at most 320 MiB of HBM per device.

```python
import math
import jax
import jax.numpy as jnp
import numpy as np
from jax import lax

D = 1536
QUERY_HEADS = 24
KEY_VALUE_HEADS = 8
HEAD_SIZE = 64
FFE = 512
TOPK = 8
SEQUENCE_TOKENS = 512
TOK_DEV = 512
TOKENS = 16384
QKV = 2560
EXPERTS = 16
MOST = 288


def packing_layout(key):
    base_key = jax.random.fold_in(key, 101)
    key_first, key_offset, key_rest = jax.random.split(base_key, 3)
    sequence_count = TOKENS // SEQUENCE_TOKENS
    shortest = SEQUENCE_TOKENS * 25 // 64
    longest = SEQUENCE_TOKENS * 125 // 32
    first_length = jax.random.randint(key_first, (sequence_count,), shortest, longest + 1)
    offset = jax.random.randint(key_offset, (sequence_count,), 0, first_length)
    rest_lengths = jax.random.randint(key_rest, (sequence_count, 3), shortest, longest + 1)
    first_length = first_length.at[0].set(longest // 2).at[1].set(longest)
    offset = offset.at[0].set(longest // 2 - 1).at[1].set(longest - SEQUENCE_TOKENS)
    rest_lengths = rest_lengths.at[0, 0].set(shortest).at[0, 1].set(shortest)
    bounds = (first_length - offset)[:, None] + jnp.concatenate([jnp.zeros((sequence_count, 1), jnp.int32), jnp.cumsum(rest_lengths, axis=1)[:, :2]], axis=1)
    within = jnp.arange(SEQUENCE_TOKENS, dtype=jnp.int32)[None, :]
    passed = (within[:, :, None] >= bounds[:, None, :]).astype(jnp.int32)
    segment = jnp.sum(passed, axis=-1).astype(jnp.int32)
    starts = jnp.concatenate([-offset[:, None], bounds], axis=1)
    start_of = jnp.take_along_axis(starts, segment, axis=1)
    position = (within - start_of).astype(jnp.int32)
    return (segment.reshape(-1), position.reshape(-1))


def draw_segments(key, part):
    return packing_layout(key)[0]


def draw_positions(key, part):
    return packing_layout(key)[1]


def level_of(own_key, extent, pieces, smallest, high):
    loudness = 1.0
    for dim, blocks in pieces:
        heights = jax.random.uniform(jax.random.fold_in(jax.random.fold_in(own_key, 6), dim), (blocks,), jnp.float32, smallest / len(pieces), high / len(pieces))
        loudness = loudness * jnp.repeat(jnp.exp(heights), extent[dim] // blocks).reshape((-1,) + (1,) * (len(extent) - 1 - dim))
    return loudness


def deal_out(stream_key, own, number, rows, count, top, bound, skew):
    ranking = jax.random.permutation(stream_key, count)
    packed, ordinary = shares(count, rows * top, bound, skew, True), shares(count, rows * top, bound, skew, False)
    places = jnp.arange(count)

    def named(tallies, turn):
        used = int((tallies > 0).sum())
        fixed = max(1, used // 4)
        shifted = fixed + (places - fixed + turn * (used - fixed)) % max(1, count - fixed)
        return jnp.zeros((count,), jnp.int32).at[ranking[jnp.where(places < fixed, places, shifted)]].set(jnp.asarray(tallies, jnp.int32))

    tallies = jnp.where(number % 4 == 0, named(packed, number // 4), named(ordinary, number - number // 4 - 1))
    mixed = jax.random.permutation(jax.random.fold_in(own, 3), count)
    source_of, taker = mixed[0:count // 2 * 2:2], mixed[1:count // 2 * 2:2]
    slack = jnp.minimum(tallies[source_of] - 1, bound - tallies[taker]) // 2
    slack = jnp.where((source_of == ranking[0]) | (taker == ranking[0]) | (tallies[taker] == 0), 0, jnp.maximum(slack, 0))
    shifted = jax.random.randint(jax.random.fold_in(own, 4), (count // 2,), 0, 1 << 20) % (slack + 1)
    tallies = tallies.at[source_of].add(-shifted).at[taker].add(shifted)
    labels = jnp.searchsorted(jnp.cumsum(tallies), jnp.arange(rows * top), side="right").astype(jnp.int32)
    grid = labels.reshape(top, rows).T
    grid = grid[jax.random.permutation(jax.random.fold_in(own, 1), rows)]
    turn = jax.random.randint(jax.random.fold_in(own, 2), (rows, 1), 0, top)
    return jnp.take_along_axis(grid, (jnp.arange(top)[None, :] + turn) % top, axis=1)


def shares(amount, total, most, skew, full):
    loads = [(1 << 20) // math.isqrt(rank ** skew) + 1 for rank in range(1, amount + 1)]
    largest = most if full else min(most, max(-(-total // amount), total * loads[0] // sum(loads)))
    least = 1 if total - largest >= amount - 1 else 0
    holding, surplus = [largest] + [least] * (amount - 1), total - largest - least * (amount - 1)
    while surplus > 0:
        movable = [i for i in range(1, amount) if holding[i] < largest] or [i for i in range(1, amount) if holding[i] < most]
        mass, remaining = sum([loads[i] for i in movable]), surplus
        for i in movable:
            more = min(most - holding[i], max(1, remaining * loads[i] // mass), surplus)
            holding[i] = holding[i] + more
            surplus = surplus - more
    return np.array(holding)


def noise(key, dims, spread, limit, shards=(), held_as=jnp.bfloat16):
    gain = level_of(key, dims, shards, -0.22, 0.18) if shards else 1.0
    result = jax.random.normal(key, dims, jnp.float32) * spread * gain
    return jnp.minimum(jnp.maximum(result, -limit), limit).astype(held_as)


def setup_inputs(seed: int = 0) -> dict:
    arg_keys = jax.random.split(jax.random.key(seed), 13)
    tokens = noise(arg_keys[0], (TOKENS, D), 1.0, 6.0, ((0, 32),))
    norm_attn = jnp.clip(1.0 + 0.1 * jax.random.normal(arg_keys[1], (D,), jnp.float32), 0.5, 1.5).astype(jnp.bfloat16)
    w_qkv = noise(arg_keys[2], (D, QKV), D ** -0.5, 0.15625, ((0, 2),))
    w_out = noise(arg_keys[3], (QUERY_HEADS * HEAD_SIZE, D), 1 ** -0.5, 6.0, ((0, 2),))
    norm_moe = jnp.clip(1.0 + 0.1 * jax.random.normal(arg_keys[4], (D,), jnp.float32), 0.5, 1.5).astype(jnp.bfloat16)
    w_router = noise(arg_keys[5], (D, EXPERTS), D ** -0.5, 0.15625, ((0, 2),))
    expert_in = noise(arg_keys[6], (EXPERTS, D, 2 * FFE), D ** -0.5, 0.15625, ((0, 16),))
    expert_out = noise(arg_keys[7], (EXPERTS, FFE, D), 4 ** -0.5, 3.0, ((0, 16),))
    routes_keys = jax.random.split(jax.random.fold_in(arg_keys[8], 1), TOKENS // TOK_DEV)
    routes_turns = jax.random.permutation(jax.random.fold_in(arg_keys[8], 3), TOKENS // TOK_DEV)
    routes = jax.vmap(lambda own, number: deal_out(jax.random.fold_in(arg_keys[8], 2), own, number, TOK_DEV, EXPERTS, TOPK, MOST, 1))(routes_keys, routes_turns).reshape((TOKENS, TOPK))
    segments = draw_segments(jax.random.fold_in(arg_keys[12], 71), 0)
    positions = draw_positions(jax.random.fold_in(arg_keys[12], 71), 0)
    cotangent = noise(arg_keys[11], (TOKENS, D), 1.0, 6.0, ((0, 32),))
    return dict(tokens=tokens, norm_attn=norm_attn, w_qkv=w_qkv, w_out=w_out, norm_moe=norm_moe, w_router=w_router, expert_in=expert_in, expert_out=expert_out, routes=routes, segments=segments, positions=positions, cotangent=cotangent)


EPSILON = 1e-06
ROPE_BASE = 10000.0
ATTN_SCALE = 0.015625
RESIDUAL_SCALE = 0.22
NEG_FILL = -1e+30

def rms_scale(values):
    return lax.rsqrt(lax.optimization_barrier(jnp.mean(values * values, axis=-1, keepdims=True)) + EPSILON)

def norm_backward(values, inv_scale, gain_vector, upstream):
    weighted = upstream * gain_vector.astype(jnp.float32)
    grad_gain = lax.optimization_barrier(jnp.sum(upstream * values * inv_scale, axis=0))
    grad_values = inv_scale * weighted - values * inv_scale ** 3 * lax.optimization_barrier(jnp.mean(values * weighted, axis=-1, keepdims=True))
    return (grad_values, grad_gain)

def rope_tables(position_ids, head_width):
    half_width = head_width // 2
    frequency = ROPE_BASE ** (-2.0 * jnp.arange(half_width, dtype=jnp.float32) / head_width)
    angles = position_ids.astype(jnp.float32)[:, None] * frequency[None, :]
    cosine = jnp.cos(angles)
    sine_table = jnp.sin(angles)
    return (jnp.concatenate([cosine, cosine], axis=1)[:, None, :], jnp.concatenate([sine_table, sine_table], axis=1)[:, None, :])

def apply_rotary_forward(values, cosine, sine_table):
    half_width = values.shape[-1] // 2
    turned = jnp.concatenate([-values[..., half_width:], values[..., :half_width]], axis=-1)
    return values * cosine + turned * sine_table

def rotate_backward(upstream, cosine, sine_table):
    half_width = upstream.shape[-1] // 2
    scaled = upstream * sine_table
    turned = jnp.concatenate([scaled[..., half_width:], -scaled[..., :half_width]], axis=-1)
    return upstream * cosine + turned

def slot_table(route_ids, expert_count, capacity):
    flat_routes = route_ids.reshape(-1)
    row_count = flat_routes.shape[0]
    onehot = (flat_routes[:, None] == jnp.arange(expert_count, dtype=jnp.int32)[None, :]).astype(jnp.int32)
    before = jnp.cumsum(onehot, axis=0) - onehot
    slot_rank = lax.optimization_barrier(jnp.sum(before * onehot, axis=1))
    target = (flat_routes * capacity + slot_rank).astype(jnp.int32)
    source = jnp.full((expert_count * capacity,), row_count, dtype=jnp.int32).at[target].set(jnp.arange(row_count, dtype=jnp.int32))
    return (target, source)

def attention_mask(segment_rows):
    length = segment_rows.shape[1]
    query_index = lax.broadcasted_iota(jnp.int32, (length, length), 0)
    key_index = lax.broadcasted_iota(jnp.int32, (length, length), 1)
    allowed = (key_index <= query_index)[None] & (segment_rows[:, :, None] == segment_rows[:, None, :])
    return allowed[:, None, None]

def layer_block(weights, block_data):
    gain_attn, qkv_weight, out_weight, gain_moe, router_weight, expert_in, expert_out = weights
    tokens_blk, routes_blk, segments_blk, positions_blk, cotangent_blk = block_data
    token_count = tokens_blk.shape[0]
    sequence_count = token_count // SEQUENCE_TOKENS
    query_group_width = QUERY_HEADS // KEY_VALUE_HEADS
    query_width = QUERY_HEADS * HEAD_SIZE
    key_value_width = KEY_VALUE_HEADS * HEAD_SIZE
    expert_count = router_weight.shape[1]
    x_in = tokens_blk.astype(jnp.float32)
    scale_attn = rms_scale(x_in)
    h_attn = (x_in * scale_attn * gain_attn.astype(jnp.float32)).astype(jnp.bfloat16)
    query_key_value_rows = jnp.dot(h_attn, qkv_weight, preferred_element_type=jnp.float32)
    cosine_lookup, sine_lookup = rope_tables(positions_blk, HEAD_SIZE)
    query_rows = apply_rotary_forward(query_key_value_rows[:, :query_width].reshape(token_count, QUERY_HEADS, HEAD_SIZE), cosine_lookup, sine_lookup).astype(jnp.bfloat16)
    rotated_key_rows = apply_rotary_forward(query_key_value_rows[:, query_width:query_width + key_value_width].reshape(token_count, KEY_VALUE_HEADS, HEAD_SIZE), cosine_lookup, sine_lookup).astype(jnp.bfloat16)
    value_rows_full = query_key_value_rows[:, query_width + key_value_width:].astype(jnp.bfloat16)
    query_rows_grouped = query_rows.reshape(sequence_count, SEQUENCE_TOKENS, KEY_VALUE_HEADS, query_group_width, HEAD_SIZE)
    key_rows_grouped = rotated_key_rows.reshape(sequence_count, SEQUENCE_TOKENS, KEY_VALUE_HEADS, HEAD_SIZE)
    value_rows_grouped = value_rows_full.reshape(sequence_count, SEQUENCE_TOKENS, KEY_VALUE_HEADS, HEAD_SIZE)
    allowed = attention_mask(segments_blk.reshape(sequence_count, SEQUENCE_TOKENS))
    scores = jnp.einsum('sqhgd,schd->shgqc', query_rows_grouped.astype(jnp.float32), key_rows_grouped.astype(jnp.float32)) * ATTN_SCALE
    scores = jnp.where(allowed, scores, NEG_FILL)
    row_max = lax.optimization_barrier(jnp.max(scores, axis=-1, keepdims=True))
    log_total = row_max + jnp.log(lax.optimization_barrier(jnp.sum(jnp.exp(scores - row_max), axis=-1, keepdims=True)))
    prob_full = jnp.exp(scores - log_total)
    probs_low = prob_full.astype(jnp.bfloat16)
    attention_output = jnp.einsum('shgqc,schd->sqhgd', probs_low.astype(jnp.float32), value_rows_grouped.astype(jnp.float32))
    attention_output = attention_output.astype(jnp.bfloat16).reshape(token_count, query_width)
    residual = x_in + RESIDUAL_SCALE * jnp.dot(attention_output, out_weight, preferred_element_type=jnp.float32)
    scale_moe = rms_scale(residual)
    h_moe = (residual * scale_moe * gain_moe.astype(jnp.float32)).astype(jnp.bfloat16)
    logits = jnp.dot(h_moe, router_weight, preferred_element_type=jnp.float32)
    chosen = jnp.take_along_axis(logits, routes_blk, axis=1)
    gate_weights = jax.nn.softmax(chosen, axis=-1)
    target, source = slot_table(routes_blk, expert_count, MOST)
    padded = jnp.concatenate([h_moe, jnp.zeros((1, D), jnp.bfloat16)], axis=0)
    send_rows = padded[source // TOPK].reshape(expert_count, MOST, D)
    projected = jnp.einsum('emd,edf->emf', send_rows.astype(jnp.float32), expert_in.astype(jnp.float32))
    gate_part = projected[..., :FFE]
    up_part = projected[..., FFE:]
    activated = (jax.nn.silu(gate_part) * up_part).astype(jnp.bfloat16)
    expert_rows = jnp.einsum('emf,efd->emd', activated.astype(jnp.float32), expert_out.astype(jnp.float32)).astype(jnp.bfloat16)
    picked = expert_rows.reshape(-1, D)[target].reshape(token_count, TOPK, D).astype(jnp.float32)
    mixed = lax.optimization_barrier(jnp.sum(gate_weights[..., None] * picked, axis=1))
    block_out = (residual + RESIDUAL_SCALE * mixed).astype(jnp.bfloat16)
    grad_out = cotangent_blk.astype(jnp.float32)
    grad_mixed = RESIDUAL_SCALE * grad_out
    grad_gates = lax.optimization_barrier(jnp.sum(picked * grad_mixed[:, None, :], axis=-1))
    grad_picked = (gate_weights[..., None] * grad_mixed[:, None, :]).astype(jnp.bfloat16).reshape(token_count * TOPK, D)
    grad_send = jnp.concatenate([grad_picked, jnp.zeros((1, D), jnp.bfloat16)], axis=0)[source].reshape(expert_count, MOST, D)
    grad_chosen = gate_weights * (grad_gates - lax.optimization_barrier(jnp.sum(gate_weights * grad_gates, axis=-1, keepdims=True)))
    selector = (routes_blk[:, :, None] == jnp.arange(expert_count, dtype=jnp.int32)[None, None, :]).astype(jnp.float32)
    grad_logits = lax.optimization_barrier(jnp.sum(selector * grad_chosen[..., None], axis=1)).astype(jnp.bfloat16)
    grad_router = jnp.dot(h_moe.T, grad_logits, preferred_element_type=jnp.float32)
    sigmoid_gate = jax.nn.sigmoid(gate_part)
    silu_gate = gate_part * sigmoid_gate
    grad_act = jnp.einsum('emd,efd->emf', grad_send.astype(jnp.float32), expert_out.astype(jnp.float32))
    grad_pre = jnp.concatenate([grad_act * up_part * sigmoid_gate * (1.0 + gate_part * (1.0 - sigmoid_gate)), grad_act * silu_gate], axis=-1).astype(jnp.bfloat16)
    grad_rows = jnp.einsum('emf,edf->emd', grad_pre.astype(jnp.float32), expert_in.astype(jnp.float32)).astype(jnp.bfloat16)
    grad_expert_in = jnp.einsum('emd,emf->edf', send_rows.astype(jnp.float32), grad_pre.astype(jnp.float32))
    grad_expert_out = jnp.einsum('emf,emd->efd', activated.astype(jnp.float32), grad_send.astype(jnp.float32))
    back_rows = grad_rows.reshape(-1, D)[target].reshape(token_count, TOPK, D).astype(jnp.float32)
    grad_h_moe = lax.optimization_barrier(jnp.sum(back_rows, axis=1)) + jnp.dot(grad_logits, router_weight.T, preferred_element_type=jnp.float32)
    grad_residual, grad_gain_moe = norm_backward(residual, scale_moe, gain_moe, grad_h_moe)
    grad_residual = grad_out + grad_residual
    grad_attn_out = (RESIDUAL_SCALE * grad_residual).astype(jnp.bfloat16)
    grad_out_weight = jnp.dot(attention_output.T, grad_attn_out, preferred_element_type=jnp.float32)
    attention_output_gradient = jnp.dot(grad_attn_out, out_weight.T, preferred_element_type=jnp.float32).astype(jnp.bfloat16)
    grouped_gradient = attention_output_gradient.reshape(sequence_count, SEQUENCE_TOKENS, KEY_VALUE_HEADS, query_group_width, HEAD_SIZE)
    attention_output_grouped = attention_output.reshape(sequence_count, SEQUENCE_TOKENS, KEY_VALUE_HEADS, query_group_width, HEAD_SIZE)
    delta_rows = lax.optimization_barrier(jnp.sum(grouped_gradient.astype(jnp.float32) * attention_output_grouped.astype(jnp.float32), axis=-1))
    delta_rows = jnp.transpose(delta_rows, (0, 2, 3, 1))[..., None]
    grad_probs = jnp.einsum('sqhgd,schd->shgqc', grouped_gradient.astype(jnp.float32), value_rows_grouped.astype(jnp.float32))
    score_gradient = (prob_full * (grad_probs - delta_rows) * ATTN_SCALE).astype(jnp.bfloat16)
    grad_query = jnp.einsum('shgqc,schd->sqhgd', score_gradient.astype(jnp.float32), key_rows_grouped.astype(jnp.float32)).reshape(token_count, QUERY_HEADS, HEAD_SIZE)
    key_gradient = jnp.einsum('xprzj,xzprk->xjpk', score_gradient.astype(jnp.float32), query_rows_grouped.astype(jnp.float32)).reshape(token_count, KEY_VALUE_HEADS, HEAD_SIZE)
    grad_values = jnp.einsum('xprzj,xzprk->xjpk', probs_low.astype(jnp.float32), grouped_gradient.astype(jnp.float32)).reshape(token_count, key_value_width)
    grad_qkv_rows = jnp.concatenate([rotate_backward(grad_query, cosine_lookup, sine_lookup).reshape(token_count, query_width), rotate_backward(key_gradient, cosine_lookup, sine_lookup).reshape(token_count, key_value_width), grad_values], axis=1).astype(jnp.bfloat16)
    grad_qkv_weight = jnp.dot(h_attn.T, grad_qkv_rows, preferred_element_type=jnp.float32)
    grad_h_attn = jnp.dot(grad_qkv_rows, qkv_weight.T, preferred_element_type=jnp.float32)
    grad_input, grad_gain_attn = norm_backward(x_in, scale_attn, gain_attn, grad_h_attn)
    grad_tokens_blk = grad_residual + grad_input
    grads = (grad_gain_attn, grad_qkv_weight, grad_out_weight, grad_gain_moe, grad_router, grad_expert_in, grad_expert_out)
    return ((block_out, grad_tokens_blk), grads)

def reference(tokens, norm_attn, w_qkv, w_out, norm_moe, w_router, expert_in, expert_out, routes, segments, positions, cotangent):
    blocks = TOKENS // TOK_DEV
    weights = (norm_attn, w_qkv, w_out, norm_moe, w_router, expert_in, expert_out)
    stacked = (tokens.reshape(blocks, TOK_DEV, D), routes.reshape(blocks, TOK_DEV, TOPK), segments.reshape(blocks, TOK_DEV), positions.reshape(blocks, TOK_DEV), cotangent.reshape(blocks, TOK_DEV, D))
    initial = (jnp.zeros((D,), jnp.float32), jnp.zeros((D, QKV), jnp.float32), jnp.zeros((QUERY_HEADS * HEAD_SIZE, D), jnp.float32), jnp.zeros((D,), jnp.float32), jnp.zeros((D, EXPERTS), jnp.float32), jnp.zeros((EXPERTS, D, 2 * FFE), jnp.float32), jnp.zeros((EXPERTS, FFE, D), jnp.float32))

    def step_fn(running, block_data):
        results, grads = layer_block(weights, block_data)
        return (tuple((total + part_grad for total, part_grad in zip(running, grads))), results)
    totals, (outputs, input_grads) = lax.scan(step_fn, initial, stacked)
    return (outputs.reshape(TOKENS, D), input_grads.reshape(TOKENS, D), totals[0], totals[1], totals[2], totals[3], totals[4], totals[5], totals[6])
```

```python
import jax
import jax.numpy as jnp
from jax import lax
from jax.experimental import pallas as pl
from jax.experimental.pallas import tpu as pltpu
from jax.sharding import PartitionSpec as P

QUERY_HEADS = 24
KEY_VALUE_HEADS = 8
HEAD_SIZE = 64
SEQUENCE_TOKENS = 512
PLANE = 4

EPSILON = 1e-06
ROPE_BASE = 10000.0
ATTN_SCALE = 0.015625
RESIDUAL_SCALE = 0.22
NEG_FILL = -1e30


BF16 = jnp.bfloat16
F32 = jnp.float32


def rms_scale(values):
    return lax.rsqrt(jnp.mean(values * values, axis=-1, keepdims=True) + EPSILON)


def norm_backward(values, inv_scale, gain_vector, upstream):
    weighted = upstream * gain_vector.astype(F32)
    grad_gain = jnp.sum(upstream * values * inv_scale, axis=0)
    grad_values = inv_scale * weighted - values * inv_scale**3 * jnp.mean(
        values * weighted, axis=-1, keepdims=True
    )
    return (grad_values, grad_gain)


def rope_tables(position_ids, head_width):
    half_width = head_width // 2
    frequency = ROPE_BASE ** (-2.0 * jnp.arange(half_width, dtype=F32) / head_width)
    angles = position_ids.astype(F32)[:, None] * frequency[None, :]
    cosine = jnp.cos(angles)
    sine_table = jnp.sin(angles)
    return (
        jnp.concatenate([cosine, cosine], axis=1)[:, None, :],
        jnp.concatenate([sine_table, sine_table], axis=1)[:, None, :],
    )


def apply_rotary_forward(values, cosine, sine_table):
    half_width = values.shape[-1] // 2
    turned = jnp.concatenate([-values[..., half_width:], values[..., :half_width]], axis=-1)
    return values * cosine + turned * sine_table


def rotate_backward(upstream, cosine, sine_table):
    half_width = upstream.shape[-1] // 2
    scaled = upstream * sine_table
    turned = jnp.concatenate([scaled[..., half_width:], -scaled[..., :half_width]], axis=-1)
    return upstream * cosine + turned


def masked_scores(query_rows_grouped, key_rows_grouped, segment_rows):
    scores = (
        jnp.einsum(
            "sqhgd,schd->shgqc",
            query_rows_grouped,
            key_rows_grouped,
            preferred_element_type=F32,
        )
        * ATTN_SCALE
    )
    length = segment_rows.shape[1]
    query_index = lax.broadcasted_iota(jnp.int32, (length, length), 0)
    key_index = lax.broadcasted_iota(jnp.int32, (length, length), 1)
    allowed = (key_index <= query_index)[None] & (
        segment_rows[:, :, None] == segment_rows[:, None, :]
    )
    return jnp.where(allowed[:, None, None], scores, NEG_FILL)


def dot(a, b, ca, cb):
    return lax.dot_general(a, b, (((ca,), (cb,)), ((), ())), preferred_element_type=F32)


class Links:
    def __init__(self):
        self.owners = lax.axis_size("expert")
        self.fsdp = lax.axis_size("fsdp")
        self.ring = self.owners // PLANE
        order = [0] + list(range(1, self.ring, 2)) + list(range(2, self.ring, 2))[::-1]
        place = [0] * self.ring
        for at, major in enumerate(order):
            place[major] = at
        index = lax.axis_index("expert")
        self.j = index % PLANE
        self.c = lax.axis_index("fsdp")
        self.order = jnp.array(order, jnp.int32)
        self.k = jnp.array(place, jnp.int32)[index // PLANE]
        self.next_pairs = [
            (order[at] * PLANE + j, order[(at + 1) % self.ring] * PLANE + j)
            for at in range(self.ring)
            for j in range(PLANE)
        ]

    def flip(self, v, bits):
        pairs = [(d, d ^ bits) for d in range(self.owners)]
        return jax.tree.map(lambda a: lax.ppermute(a, "expert", pairs), v)

    def onward(self, v):
        return jax.tree.map(lambda a: lax.ppermute(a, "expert", self.next_pairs), v)

    def from_core(self, v, shift):
        n = self.fsdp
        pairs = [(s, (s - shift) % n) for s in range(n)]
        return jax.tree.map(lambda a: lax.ppermute(a, "fsdp", pairs), v)

    def join(self, w):
        if self.fsdp != 2:
            return lax.all_gather(w, "fsdp", axis=0, tiled=True)
        other = self.from_core(w, 1)
        first = jnp.where(self.c == 0, w, other)
        second = jnp.where(self.c == 0, other, w)
        return jnp.concatenate([first, second], axis=0)

    def plane_gather(self, v):
        half = v.shape[0] // 2
        vx = self.flip(v, 1)
        vy = self.flip(v, 2)
        d0 = self.flip(vx[:half], 2)
        d1 = self.flip(vy[half:], 1)
        return v, vx, vy, jnp.concatenate([d0, d1], axis=0)

    def plane_reduce(self, parts):
        own, px, py, pd = parts
        half = own.shape[0] // 2
        s0 = self.flip(pd[:half].astype(BF16), 1)
        s1 = self.flip(pd[half:].astype(BF16), 2)
        py = jnp.concatenate([py[:half].astype(F32) + s0.astype(F32), py[half:].astype(F32)], 0)
        px = jnp.concatenate([px[:half].astype(F32), px[half:].astype(F32) + s1.astype(F32)], 0)
        rx = self.flip(px.astype(BF16), 1)
        ry = self.flip(py.astype(BF16), 2)
        return own.astype(F32) + rx.astype(F32) + ry.astype(F32)

    def ring_reduce(self, part_of):
        acc = part_of(1 % self.ring)
        for s in range(1, self.ring):
            got = self.onward(jax.tree.map(lambda a: a.astype(BF16), acc))
            acc = jax.tree.map(
                lambda g, p: g.astype(F32) + p.astype(F32), got, part_of((s + 1) % self.ring)
            )
        return acc

    def reduce_all(self, m):
        rows = m.shape[0]
        q = rows // PLANE
        z = q // self.ring

        def piece(b):
            return lax.dynamic_slice_in_dim(m, (self.j ^ b) * q, q, 0)

        s = self.plane_reduce([piece(b) for b in range(PLANE)])

        def chunk(back):
            return lax.dynamic_slice_in_dim(s, ((self.k - back) % self.ring) * z, z, 0)

        acc = self.ring_reduce(chunk).astype(BF16)
        full = jnp.zeros(s.shape, BF16)
        for r in range(self.ring):
            full = lax.dynamic_update_slice_in_dim(
                full, acc, ((self.k - r) % self.ring) * z, 0
            )
            if r + 1 < self.ring:
                acc = self.onward(acc)
        blocks = self.plane_gather(full)
        out = jnp.zeros(m.shape, F32)
        for b in range(PLANE):
            out = lax.dynamic_update_slice_in_dim(
                out, blocks[b].astype(F32), (self.j ^ b) * q, 0
            )
        return out

    def reduce_small(self, m):
        bits = 1
        while bits < self.owners:
            m = m + self.flip(m.astype(BF16), bits).astype(F32)
            bits *= 2
        return m


def expert_body(slot, parts, fh, more, gates_ref, h_ref, c_ref, *refs):
    win = refs[:parts]
    wout = refs[parts : 2 * parts]
    refs = refs[2 * parts :]
    if more:
        dh_in, out_in = refs[:2]
        refs = refs[2:]
    dpre_ref, ga_ref, dg_ref, dh_ref, out_ref = refs
    h = h_ref[...]
    c = c_ref[...]
    gate = gates_ref[:, slot : slot + 1]
    total = jnp.zeros(gate.shape, F32)
    for q in range(parts):
        p = jnp.dot(h, win[q][...], preferred_element_type=F32)
        z = dot(c, wout[q][...], 1, 1)
        g = p[:, :fh]
        u = p[:, fh:]
        sg = 1.0 / (1.0 + jnp.exp(-g))
        silu = g * sg
        act = silu * u
        total = total + jnp.sum(z * act, axis=-1, keepdims=True)
        da = (RESIDUAL_SCALE * gate) * z
        at = q * 2 * fh
        dpre_ref[:, at : at + fh] = (da * u * sg * (1.0 + g * (1.0 - sg))).astype(BF16)
        dpre_ref[:, at + fh : at + 2 * fh] = (da * silu).astype(BF16)
        ga_ref[:, q * fh : (q + 1) * fh] = (gate * act).astype(BF16)
    dg_ref[...] = RESIDUAL_SCALE * total
    dh = dh_in[...] if more else None
    out = out_in[...] if more else None
    for q in range(parts):
        a = dot(dpre_ref[:, q * 2 * fh : (q + 1) * 2 * fh], win[q][...], 1, 1)
        o = dot(ga_ref[:, q * fh : (q + 1) * fh], wout[q][...], 1, 0)
        dh = a if dh is None else dh + a
        out = o if out is None else out + o
    dh_ref[...] = dh
    out_ref[...] = out


def expert_call(slot, gates, h, c, win, wout, sums, tile=256):
    tokens, width = h.shape
    parts = len(win)
    fh = wout[0].shape[0]
    more = bool(sums)

    def rows(n):
        return pl.BlockSpec((tile, n), lambda t: (t, 0))

    def whole(a):
        return pl.BlockSpec(a.shape, lambda t: (0, 0))

    def body(*refs):
        expert_body(slot, parts, fh, more, *refs)

    base = 3 + 2 * parts
    return pl.pallas_call(
        body,
        grid=(tokens // tile,),
        in_specs=[rows(gates.shape[1]), rows(width), rows(width)]
        + [whole(w) for w in win]
        + [whole(w) for w in wout]
        + [rows(width) for _ in sums],
        out_specs=[rows(parts * 2 * fh), rows(parts * fh), rows(1), rows(width), rows(width)],
        out_shape=[
            jax.ShapeDtypeStruct((tokens, parts * 2 * fh), BF16),
            jax.ShapeDtypeStruct((tokens, parts * fh), BF16),
            jax.ShapeDtypeStruct((tokens, 1), F32),
            jax.ShapeDtypeStruct((tokens, width), F32),
            jax.ShapeDtypeStruct((tokens, width), F32),
        ],
        input_output_aliases={base: 3, base + 1: 4} if more else {},
        name=f"expert_{slot}",
    )(gates, h, c, *win, *wout, *sums)


def weight_grads_body(blocks, order, fh, _, *refs):
    h = refs[:blocks]
    c = refs[blocks : 2 * blocks]
    pre = refs[2 * blocks : 3 * blocks]
    act = refs[3 * blocks : 4 * blocks]
    gi_ref, go_ref = refs[4 * blocks :]
    for at, q in enumerate(order):
        gi = go = None
        for b in range(blocks):
            i = dot(h[b][...], pre[b][:, q * 2 * fh : (q + 1) * 2 * fh], 0, 0)
            o = dot(act[b][:, q * fh : (q + 1) * fh], c[b][...], 0, 0)
            gi = i if gi is None else gi + i
            go = o if go is None else go + o
        gi_ref[:, at * 2 * fh : (at + 1) * 2 * fh] = gi.astype(BF16)
        go_ref[at * fh : (at + 1) * fh, :] = (RESIDUAL_SCALE * go).astype(BF16)


def weight_grads_call(chunk, order, dc, fh, h, c, pre, act):
    blocks = len(h)
    tokens = h[0].shape[0]
    parts = len(order)

    def share(n):
        return pl.BlockSpec((tokens, n), lambda t, ref: (0, ref[0]))

    def whole(a):
        return pl.BlockSpec(a.shape, lambda t, ref: (0, 0))

    def body(*refs):
        weight_grads_body(blocks, order, fh, *refs)

    return pl.pallas_call(
        body,
        grid_spec=pltpu.PrefetchScalarGridSpec(
            num_scalar_prefetch=1,
            grid=(1,),
            in_specs=[share(dc)] * (2 * blocks) + [whole(v) for v in (*pre, *act)],
            out_specs=[
                pl.BlockSpec((dc, parts * 2 * fh), lambda t, ref: (0, 0)),
                pl.BlockSpec((parts * fh, dc), lambda t, ref: (0, 0)),
            ],
        ),
        out_shape=[
            jax.ShapeDtypeStruct((dc, parts * 2 * fh), BF16),
            jax.ShapeDtypeStruct((parts * fh, dc), BF16),
        ],
        name="weight_grads",
    )(chunk.reshape(1), *h, *c, *pre, *act)


def per_device(
    tokens,
    norm_attn,
    w_qkv,
    w_out,
    norm_moe,
    w_router,
    expert_in,
    expert_out,
    routes,
    segments,
    positions,
    cotangent,
):
    ln = Links()
    fsdp, ring, owners = ln.fsdp, ln.ring, ln.owners
    token_count, model_width = tokens.shape
    ffe = expert_out.shape[1]
    fh = ffe // fsdp
    dc = model_width // fsdp

    def hidden_share(p):
        at = ((ln.c + p) % fsdp) * fh
        g = lax.dynamic_slice_in_dim(expert_in[0], at, fh, 1)
        u = lax.dynamic_slice_in_dim(expert_in[0], at + ffe, fh, 1)
        return jnp.concatenate([g, u], axis=1), lax.dynamic_slice_in_dim(expert_out[0], at, fh, 0)

    slots = [[hidden_share(p) for p in range(fsdp)]]
    moving = slots[0][0]
    for _ in range(1, ring):
        moving = ln.onward(moving)
        slots.append([moving] + [ln.from_core(moving, p) for p in range(1, fsdp)])

    cot_blocks = ln.plane_gather(cotangent)
    gain_attn, qkv_weight, out_weight, gain_moe, router_weight = (
        ln.join(norm_attn),
        ln.join(w_qkv),
        ln.join(w_out),
        ln.join(norm_moe),
        ln.join(w_router),
    )
    experts = router_weight.shape[1]
    sequence_count = token_count // SEQUENCE_TOKENS
    query_group_width = QUERY_HEADS // KEY_VALUE_HEADS
    query_width = QUERY_HEADS * HEAD_SIZE
    key_value_width = KEY_VALUE_HEADS * HEAD_SIZE
    x_in = tokens.astype(F32)
    scale_attn = rms_scale(x_in)
    h_attn = (x_in * scale_attn * gain_attn.astype(F32)).astype(BF16)
    query_key_value_rows = jnp.dot(h_attn, qkv_weight, preferred_element_type=F32)
    cosine_lookup, sine_lookup = rope_tables(positions, HEAD_SIZE)
    query_rows = apply_rotary_forward(
        query_key_value_rows[:, :query_width].reshape(token_count, QUERY_HEADS, HEAD_SIZE),
        cosine_lookup,
        sine_lookup,
    ).astype(BF16)
    rotated_key_rows = apply_rotary_forward(
        query_key_value_rows[:, query_width : query_width + key_value_width].reshape(
            token_count, KEY_VALUE_HEADS, HEAD_SIZE
        ),
        cosine_lookup,
        sine_lookup,
    ).astype(BF16)
    value_rows_full = query_key_value_rows[:, query_width + key_value_width :].astype(BF16)
    query_rows_grouped = query_rows.reshape(
        sequence_count, SEQUENCE_TOKENS, KEY_VALUE_HEADS, query_group_width, HEAD_SIZE
    )
    key_rows_grouped = rotated_key_rows.reshape(
        sequence_count, SEQUENCE_TOKENS, KEY_VALUE_HEADS, HEAD_SIZE
    )
    value_rows_grouped = value_rows_full.reshape(
        sequence_count, SEQUENCE_TOKENS, KEY_VALUE_HEADS, HEAD_SIZE
    )
    segment_rows = segments.reshape(sequence_count, SEQUENCE_TOKENS)
    scores = masked_scores(query_rows_grouped, key_rows_grouped, segment_rows)
    row_max = jnp.max(scores, axis=-1, keepdims=True)
    log_total = row_max + jnp.log(jnp.sum(jnp.exp(scores - row_max), axis=-1, keepdims=True))
    probs_low = jnp.exp(scores - log_total).astype(BF16)
    attention_output = jnp.einsum(
        "shgqc,schd->sqhgd", probs_low, value_rows_grouped, preferred_element_type=F32
    )
    attention_output = attention_output.astype(BF16).reshape(token_count, query_width)
    residual = x_in + RESIDUAL_SCALE * jnp.dot(
        attention_output, out_weight, preferred_element_type=F32
    )
    scale_moe = rms_scale(residual)
    h_moe = (residual * scale_moe * gain_moe.astype(F32)).astype(BF16)

    h_blocks = ln.plane_gather(h_moe)
    logits = dot(router_weight, h_moe, 0, 1)
    chosen = jnp.any(
        routes.T[:, None, :] == jnp.arange(experts, dtype=jnp.int32)[None, :, None], axis=0
    )
    logits = jnp.where(chosen, logits, NEG_FILL)
    weights = jnp.where(chosen, jnp.exp(logits - jnp.max(logits, axis=0, keepdims=True)), 0.0)
    gates = weights / jnp.sum(weights, axis=0, keepdims=True)
    gate_blocks = [gates] + [ln.flip(gates, b) for b in range(1, PLANE)]

    slot_major = ln.order[(ln.k - jnp.arange(ring)) % ring]
    pick = [
        (
            (slot_major * PLANE + (ln.j ^ b))[:, None]
            == jnp.arange(experts, dtype=jnp.int32)[None, :]
        ).astype(F32)
        for b in range(PLANE)
    ]
    my_gates = [
        lax.dot_general(
            g,
            pick[0],
            (((0,), (1,)), ((), ())),
            precision=lax.Precision.HIGHEST,
            preferred_element_type=F32,
        )
        for g in gate_blocks
    ]

    pre, act, dgate = [], [], [[] for _ in range(PLANE)]
    sums = [() for _ in range(PLANE)]
    for s in range(ring):
        pre.append([None] * PLANE)
        act.append([None] * PLANE)
        for b in (0, 1, 2, 3) if s + 1 < ring else (3, 1, 2, 0):
            pre[s][b], act[s][b], d, *sums[b] = expert_call(
                s,
                my_gates[b],
                h_blocks[b],
                cot_blocks[b],
                [w[0] for w in slots[s]],
                [w[1] for w in slots[s]],
                sums[b],
            )
            dgate[b].append(d)
    back = ln.plane_reduce([s[0] for s in sums])
    dgate_blocks = [jnp.concatenate(d, axis=1).T for d in dgate]
    dgate_got = [dgate_blocks[0]] + [ln.flip(dgate_blocks[b], b) for b in range(1, PLANE)]
    grad_gates = lax.dot_general(
        jnp.concatenate(pick, axis=0),
        jnp.concatenate(dgate_got, axis=0),
        (((0,), (0,)), ((), ())),
        precision=lax.Precision.HIGHEST,
        preferred_element_type=F32,
    )

    def width_share(v, p):
        return lax.dynamic_slice_in_dim(v, ((ln.c + p) % fsdp) * dc, dc, 1)

    def slot_grads(s):
        total = None
        for p in list(range(1, fsdp)) + [0]:
            order = [(p + q) % fsdp for q in range(fsdp)]
            gi, go = weight_grads_call(
                (ln.c + p) % fsdp, order, dc, fh, h_blocks, cot_blocks, pre[s], act[s]
            )
            if p:
                gi, go = ln.from_core((gi, go), fsdp - p)
            total = (
                (gi, go)
                if total is None
                else (total[0].astype(F32) + gi.astype(F32), total[1].astype(F32) + go.astype(F32))
            )
        return total

    grad_in, grad_out_w = ln.ring_reduce(slot_grads)
    gates_part = [grad_in[:, q * 2 * fh : q * 2 * fh + fh] for q in range(fsdp)]
    ups_part = [grad_in[:, q * 2 * fh + fh : (q + 1) * 2 * fh] for q in range(fsdp)]

    def ordered(v, axis):
        out = jnp.zeros_like(jnp.concatenate(v, axis=axis))
        for q in range(fsdp):
            out = lax.dynamic_update_slice_in_dim(out, v[q], ((ln.c + q) % fsdp) * fh, axis)
        return out

    grad_expert_in = jnp.concatenate([ordered(gates_part, 1), ordered(ups_part, 1)], axis=1)[None]
    grad_expert_out = ordered([grad_out_w[q * fh : (q + 1) * fh] for q in range(fsdp)], 0)[None]

    mixed = ln.plane_reduce([s[1] for s in sums])
    block_out = (residual + RESIDUAL_SCALE * mixed).astype(BF16)

    grad_out = cotangent.astype(F32)
    grad_logits = (
        gates * (grad_gates - jnp.sum(gates * grad_gates, axis=0, keepdims=True))
    ).astype(BF16)
    grad_h_moe = back + dot(grad_logits, router_weight, 0, 1)
    grad_router_local = dot(grad_logits, h_moe, 1, 0)
    grad_residual, grad_gain_moe = norm_backward(residual, scale_moe, gain_moe, grad_h_moe)
    grad_residual = grad_out + grad_residual
    grad_attn_out = (RESIDUAL_SCALE * grad_residual).astype(BF16)
    attention_output_gradient = dot(grad_attn_out, out_weight, 1, 1).astype(BF16)
    grouped_gradient = attention_output_gradient.reshape(
        sequence_count, SEQUENCE_TOKENS, KEY_VALUE_HEADS, query_group_width, HEAD_SIZE
    )
    attention_output_grouped = attention_output.reshape(
        sequence_count, SEQUENCE_TOKENS, KEY_VALUE_HEADS, query_group_width, HEAD_SIZE
    )

    def reduce_rows(lhs, rhs):
        total = None
        for p in list(range(1, fsdp)) + [0]:
            g = dot(width_share(lhs, p), rhs, 0, 0)
            if p:
                g = ln.from_core(g.astype(BF16), fsdp - p)
            total = g if total is None else total.astype(F32) + g.astype(F32)
        return ln.reduce_all(total)

    total_out_proj = reduce_rows(attention_output, grad_attn_out)

    scores = masked_scores(query_rows_grouped, key_rows_grouped, segment_rows)
    prob_full = jnp.exp(scores - log_total)
    probs_again = prob_full.astype(BF16)
    delta_rows = jnp.sum(
        grouped_gradient.astype(F32) * attention_output_grouped.astype(F32), axis=-1
    )
    delta_rows = jnp.transpose(delta_rows, (0, 2, 3, 1))[..., None]
    grad_probs = jnp.einsum(
        "sqhgd,schd->shgqc",
        grouped_gradient,
        value_rows_grouped,
        preferred_element_type=F32,
    )
    score_gradient = (prob_full * (grad_probs - delta_rows) * ATTN_SCALE).astype(BF16)
    grad_query = jnp.einsum(
        "shgqc,schd->sqhgd", score_gradient, key_rows_grouped, preferred_element_type=F32
    ).reshape(token_count, QUERY_HEADS, HEAD_SIZE)
    key_gradient = jnp.einsum(
        "xprzj,xzprk->xjpk", score_gradient, query_rows_grouped, preferred_element_type=F32
    ).reshape(token_count, KEY_VALUE_HEADS, HEAD_SIZE)
    grad_values = jnp.einsum(
        "xprzj,xzprk->xjpk", probs_again, grouped_gradient, preferred_element_type=F32
    ).reshape(token_count, key_value_width)
    grad_qkv_rows = jnp.concatenate(
        [
            rotate_backward(grad_query, cosine_lookup, sine_lookup).reshape(
                token_count, query_width
            ),
            rotate_backward(key_gradient, cosine_lookup, sine_lookup).reshape(
                token_count, key_value_width
            ),
            grad_values,
        ],
        axis=1,
    ).astype(BF16)
    total_qkv = reduce_rows(h_attn, grad_qkv_rows)
    grad_h_attn = dot(grad_qkv_rows, qkv_weight, 1, 1)
    grad_input, grad_gain_attn = norm_backward(x_in, scale_attn, gain_attn, grad_h_attn)
    grad_tokens = grad_residual + grad_input

    small = jnp.concatenate(
        [grad_router_local, grad_gain_moe[None], grad_gain_attn[None]], axis=0
    )
    mine = width_share(small, 0)
    for p in range(1, fsdp):
        mine = mine + ln.from_core(width_share(small, p).astype(BF16), fsdp - p).astype(F32)
    mine = ln.reduce_small(mine)
    return (
        block_out,
        grad_tokens,
        mine[experts + 1],
        total_qkv,
        total_out_proj,
        mine[experts],
        mine[:experts].T,
        grad_expert_in,
        grad_expert_out,
    )


def solution(mesh):
    return jax.shard_map(
        per_device,
        mesh=mesh,
        in_specs=(
            P(("fsdp", "expert"), None),
            P("fsdp"),
            P("fsdp", None),
            P("fsdp", None),
            P("fsdp"),
            P("fsdp", None),
            P("expert", None, None),
            P("expert", None, None),
            P(("fsdp", "expert"), None),
            P(("fsdp", "expert")),
            P(("fsdp", "expert")),
            P(("fsdp", "expert"), None),
        ),
        out_specs=(
            P(("fsdp", "expert"), None),
            P(("fsdp", "expert"), None),
            P("fsdp"),
            P("fsdp", None),
            P("fsdp", None),
            P("fsdp"),
            P("fsdp", None),
            P("expert", "fsdp", None),
            P("expert", None, "fsdp"),
        ),
        check_vma=False,
    )
```
